32 devices in a mesh: frame: 16 (over z, y, core), head: 2 (over x).
Axes of the slice: x: 2, y: 2, z: 4, core: 2. Of those that a mesh axis runs over, the one named last changes fastest.
Arguments:
- tokens: bfloat16 [16384, 3072], P('frame'), may hold values from -6 to 6
- qkv_weight: bfloat16 [3, 3072, 3072], P(None, None, 'head'), may hold values from -0.109375 to 0.109375
- query_gain: float32 [128], replicated, may hold values from 0.1 to 1.9
- key_gain: float32 [128], replicated, may hold values from 0.1 to 1.9
- labels: int32 [24], P('head'), may hold values from 0 to 1, as said below
- space_mask: int32 [24, 16, 48], P('head'), may hold values from 0 to 1, as said below
- time_mask: int32 [24, 2, 2], P('head'), may hold values from 0 to 1, as said below
Outputs:
- attended: bfloat16 [16384, 3072], P(('frame', 'head'))
The draws below stay inside these ranges and needn't reach their ends.
Inputs may be any that keep to these rules, and one draw needn't show every extreme that they name: `labels`: among heads 3 * j, 3 * j + 1 and 3 * j + 2 exactly one is temporal. space_mask[h, a, 16 + a] = 1 for every head and query block. For each head, at most 8 key blocks of the previous frame (b < 16) are allowed for some query block, and at most 8 of the next frame (b >= 32); some head reaches 8 on each side. time_mask[h, a, a] = 1 for every head and query block.
All inputs are finite; a program needn't handle non-finite values.
Results may differ from the reference program's by a relative error of at most 0.0073.
Values may be sent and summed in bfloat16 or wider, within the bound.
A program may use at most 192 MiB of HBM per device.

```python
import math
import jax
import jax.numpy as jnp
from jax import lax

D = 3072
HEADS = 24
HEAD_DIM = 128
TOK_FRAME = 1024
STRIP = 8
BLOCK = 64
FRAMES = 16
TOKENS = 16384
QBLOCKS = 16
TBLOCKS = 2
NEAR_MAX = 8


def draw_labels(key, part):
    groups = HEADS // 3
    chosen = jax.random.randint(key, (groups,), 0, 3)
    marks = jnp.arange(3, dtype=jnp.int32)[None, :] == chosen[:, None]
    return marks.astype(jnp.int32).reshape(HEADS)


def draw_space_mask(key, part):
    keys = jax.random.split(jax.random.fold_in(key, 11), 7)
    density = jax.random.randint(keys[0], (HEADS, 1, 1), 2, 9)
    middle = jax.random.randint(keys[1], (HEADS, QBLOCKS, QBLOCKS), 0, 10) < density
    diagonal = jnp.eye(QBLOCKS, dtype=jnp.int32)[None] == 1
    middle = middle | diagonal
    counts = jax.random.randint(keys[2], (2, HEADS), 1, NEAR_MAX + 1)
    fullest = jax.random.randint(keys[3], (2,), 0, HEADS)
    counts = jnp.where(jnp.arange(HEADS, dtype=jnp.int32)[None, :] == fullest[:, None], NEAR_MAX, counts)
    scores = jax.random.randint(keys[4], (2, HEADS, QBLOCKS), 0, 1 << 20) * QBLOCKS + jnp.arange(QBLOCKS, dtype=jnp.int32)
    ranking = jnp.argsort(jnp.argsort(scores, axis=-1), axis=-1)
    column_on = ranking < counts[:, :, None]
    random_live = jax.random.randint(keys[5], (2, HEADS, QBLOCKS, QBLOCKS), 0, 10) < density[None]
    forced_row = jax.random.randint(keys[6], (2, HEADS, QBLOCKS), 0, QBLOCKS)
    row_ids = jnp.arange(QBLOCKS, dtype=jnp.int32)[None, None, :, None]
    forced = row_ids == forced_row[:, :, None, :]
    near = column_on[:, :, None, :] & (random_live | forced)
    whole = jnp.concatenate([near[0], middle, near[1]], axis=2)
    return whole.astype(jnp.int32)


def draw_time_mask(key, part):
    keys = jax.random.split(jax.random.fold_in(key, 23), 2)
    density = jax.random.randint(keys[0], (HEADS, 1, 1), 2, 9)
    live = jax.random.randint(keys[1], (HEADS, TBLOCKS, TBLOCKS), 0, 10) < density
    live = live | (jnp.eye(TBLOCKS, dtype=jnp.int32)[None] == 1)
    return live.astype(jnp.int32)


def shard_levels(stream_key, shape, shards, least, high):
    loudness = 1.0
    for position, blocks in shards:
        heights = jax.random.uniform(jax.random.fold_in(jax.random.fold_in(stream_key, 6), position), (blocks,), jnp.float32, least / len(shards), high / len(shards))
        loudness = loudness * jnp.repeat(jnp.exp(heights), shape[position] // blocks).reshape((-1,) + (1,) * (len(shape) - 1 - position))
    return loudness


def gaussian(rng, dims, scale, most, cuts=(), held_as=jnp.bfloat16):
    values = scale * jax.random.normal(rng, dims, jnp.float32)
    if cuts:
        values = values * shard_levels(rng, dims, cuts, -0.22, 0.18)
    return jnp.clip(values, -most, most).astype(held_as)


def setup_inputs(seed: int = 0) -> dict:
    arg_keys = jax.random.split(jax.random.key(seed), 8)
    tokens = gaussian(arg_keys[0], (TOKENS, D), 1.0, 6.0, ((0, 16),))
    qkv_weight = gaussian(arg_keys[1], (3, D, HEADS * HEAD_DIM), D ** -0.5, 0.109375, ((2, 2),))
    query_gain = jnp.clip(1.0 + 0.18 * jax.random.normal(arg_keys[2], (HEAD_DIM,), jnp.float32), 0.1, 1.9)
    key_gain = jnp.clip(1.0 + 0.18 * jax.random.normal(arg_keys[3], (HEAD_DIM,), jnp.float32), 0.1, 1.9)
    labels = draw_labels(jax.random.fold_in(arg_keys[7], 71), 0)
    space_mask = draw_space_mask(jax.random.fold_in(arg_keys[7], 71), 0)
    time_mask = draw_time_mask(jax.random.fold_in(arg_keys[7], 71), 0)
    return dict(tokens=tokens, qkv_weight=qkv_weight, query_gain=query_gain, key_gain=key_gain, labels=labels, space_mask=space_mask, time_mask=time_mask)


epsilon = 1e-06

def normed(projected, gains):
    inverse_rms = lax.rsqrt(lax.optimization_barrier(jnp.mean(projected * projected, axis=-1, keepdims=True)) + epsilon)
    return (projected * inverse_rms * gains).astype(jnp.bfloat16)

def expand(block_mask):
    widened = jnp.repeat(block_mask.astype(jnp.float32), BLOCK, axis=-2)
    return jnp.repeat(widened, BLOCK, axis=-1)

def attend(queries, key_rows, values, allowed):
    scores = jnp.einsum('...rd,...cd->...rc', queries.astype(jnp.float32), key_rows.astype(jnp.float32)) / math.sqrt(HEAD_DIM)
    weight = jnp.exp(scores) * allowed
    denominator = lax.optimization_barrier(jnp.sum(weight, axis=-1, keepdims=True))
    rounded = lax.optimization_barrier(weight.astype(jnp.bfloat16)).astype(jnp.float32)
    return jnp.einsum('...rc,...cd->...rd', rounded, values.astype(jnp.float32)) / denominator

def space_head(queries, key_rows, values, space_live, time_live):
    blank = jnp.zeros((1, TOK_FRAME, HEAD_DIM), jnp.bfloat16)
    padded_keys = jnp.concatenate([blank, key_rows, blank], axis=0)
    padded_values = jnp.concatenate([blank, values, blank], axis=0)
    window_keys = jnp.concatenate([padded_keys[:-2], padded_keys[1:-1], padded_keys[2:]], axis=1)
    window_values = jnp.concatenate([padded_values[:-2], padded_values[1:-1], padded_values[2:]], axis=1)
    frame_ids = jnp.arange(FRAMES, dtype=jnp.int32)
    lower_ok = (frame_ids > 0).astype(jnp.float32)
    upper_ok = (frame_ids < FRAMES - 1).astype(jnp.float32)
    ones_row = jnp.ones((FRAMES, QBLOCKS), jnp.float32)
    reach = jnp.concatenate([ones_row * lower_ok[:, None], ones_row, ones_row * upper_ok[:, None]], axis=1)

    def one_frame(frame_items):
        frame_q, frame_k, frame_v, frame_reach = frame_items
        allowed = expand(space_live.astype(jnp.float32) * frame_reach[None, :])
        return attend(frame_q, frame_k, frame_v, allowed)
    return lax.map(one_frame, (queries, window_keys, window_values, reach))

def to_strips(whole):
    strip_count = TOK_FRAME // STRIP
    shaped = whole.reshape(FRAMES, strip_count, STRIP, HEAD_DIM).transpose(1, 0, 2, 3)
    return shaped.reshape(strip_count, FRAMES * STRIP, HEAD_DIM)

def time_head(queries, key_rows, values, space_live, time_live):
    strip_count = TOK_FRAME // STRIP
    allowed = expand(time_live)[None]
    result = attend(to_strips(queries), to_strips(key_rows), to_strips(values), allowed)
    result = result.reshape(strip_count, FRAMES, STRIP, HEAD_DIM).transpose(1, 0, 2, 3)
    return result.reshape(FRAMES, TOK_FRAME, HEAD_DIM)

def reference(tokens, qkv_weight, query_gain, key_gain, labels, space_mask, time_mask):

    def project(index):
        product = jnp.dot(tokens, qkv_weight[index], preferred_element_type=jnp.float32)
        return product.reshape(FRAMES, TOK_FRAME, HEADS, HEAD_DIM)
    queries = normed(project(0), query_gain).transpose(2, 0, 1, 3)
    key_rows = normed(project(1), key_gain).transpose(2, 0, 1, 3)
    values = project(2).astype(jnp.bfloat16).transpose(2, 0, 1, 3)

    def one_head(head_items):
        head_q, head_k, head_v, label, space_live, time_live = head_items
        return lax.cond(label == 1, time_head, space_head, head_q, head_k, head_v, space_live, time_live)
    mixed = lax.map(one_head, (queries, key_rows, values, labels, space_mask, time_mask))
    return mixed.transpose(1, 2, 0, 3).reshape(TOKENS, HEADS * HEAD_DIM).astype(jnp.bfloat16)
```

```python
import functools
import math

import jax
import jax.numpy as jnp
from jax import lax
from jax.experimental import pallas as pl
from jax.experimental.pallas import tpu as pltpu
from jax.sharding import PartitionSpec as P


STRIP = 8
BLOCK = 64
NEAR_MAX = 8
HD = 128
epsilon = 1e-06
BIG = 1e30
VMEM_LIMIT = 56 * 1024 * 1024


def chunk_rows(rows, want):
    while rows % want:
        want //= 2
    return want


def normed_head(projected, gains):
    inverse_rms = lax.rsqrt(jnp.mean(projected * projected, axis=-1, keepdims=True) + epsilon)
    return (projected * inverse_rms * gains).astype(jnp.bfloat16)


def project_kernel(kinds, pair, near_count, strips, table, x_ref, gq_ref, gk_ref, after_ref, *refs):
    weights = refs[: len(kinds) * pair]
    outs = refs[len(kinds) * pair :]
    out_ref = outs[0]
    i = pl.program_id(0)
    count = pl.num_programs(0) * pair
    step = x_ref.shape[0] // strips if strips > 1 else chunk_rows(x_ref.shape[0], 512)
    gains = {0: gq_ref[...], 1: gk_ref[...]}

    def body(m, carry):
        rows = pl.ds(pl.multiple_of(m * step, step), step)
        x = x_ref[rows, :]
        for n, kind in enumerate(kinds):
            w = [w_ref[...] for w_ref in weights[n * pair : (n + 1) * pair]]
            w = w[0] if pair == 1 else jnp.concatenate(w, axis=1)
            product = jnp.dot(x, w, preferred_element_type=jnp.float32)
            for j in range(pair):
                part = product[:, j * HD : (j + 1) * HD]
                if kind in gains:
                    part = normed_head(part, gains[kind])
                else:
                    part = part.astype(jnp.bfloat16)
                if strips:
                    pos = out_ref.shape[3]
                    if strips == 1:
                        per = step // pos
                        out_ref[pl.ds(m * per, per), n, j] = part.reshape(per, pos, HD)
                    else:
                        q = pos // strips
                        at = pl.ds(pl.multiple_of(m * q, q), q)
                        out_ref[:, n, j, at, :] = part.reshape(out_ref.shape[0], q, HD)
                else:
                    out_ref[n, j, rows, :] = part
        return carry

    lax.fori_loop(0, x_ref.shape[0] // step, body, 0)
    for j in range(pair if near_count else 0):
        head = i * pair + j
        for s in range(near_count):
            for side, ref in ((0, outs[1]), (1, outs[2])):
                b = table[count + (head * 2 + side) * near_count + s]
                src = pl.ds(pl.multiple_of(b * BLOCK, BLOCK), BLOCK)
                for n in range(2):
                    ref[n, j, s * BLOCK : (s + 1) * BLOCK, :] = out_ref[n, j, src, :]


def project(tokens, weight, gq, gk, heads, kinds, after, strips=0, deal=1, picks=None):
    rows, d = tokens.shape
    count = heads.shape[0]
    pair = 2 if count % 2 == 0 else 1
    n = len(kinds)
    near_count = 0 if picks is None else NEAR_MAX
    table = heads if picks is None else jnp.concatenate([heads, picks.reshape(-1)])

    def w_spec(kind, j):
        return pl.BlockSpec((None, d, HD), lambda i, t: (kind, 0, t[pair * i + j]))

    gain = pl.BlockSpec((1, HD), lambda i, t: (0, 0))
    if strips:
        pos = rows // strips
        shapes = [jax.ShapeDtypeStruct((strips, n, count, pos, HD), jnp.bfloat16)]
        specs = [pl.BlockSpec((strips, n, pair, pos, HD), lambda i, t: (0, 0, i, 0, 0))]
    else:
        shapes = [jax.ShapeDtypeStruct((n, count, rows, HD), jnp.bfloat16)]
        specs = [pl.BlockSpec((n, pair, rows, HD), lambda i, t: (0, i, 0, 0))]
    if near_count:
        near = near_count * BLOCK
        shapes += [jax.ShapeDtypeStruct((2, count, near, HD), jnp.bfloat16)] * 2
        specs += [pl.BlockSpec((2, pair, near, HD), lambda i, t: (0, i, 0, 0))] * 2
    out = pl.pallas_call(
        functools.partial(project_kernel, kinds, pair, near_count, deal if strips else 0),
        out_shape=tuple(shapes),
        grid_spec=pltpu.PrefetchScalarGridSpec(
            num_scalar_prefetch=1,
            grid=(count // pair,),
            in_specs=[
                pl.BlockSpec((rows, d), lambda i, t: (0, 0), pipeline_mode=pl.Buffered(1)),
                gain,
                gain,
                pl.BlockSpec(memory_space=pl.ANY),
            ]
            + [w_spec(kind, j) for kind in kinds for j in range(pair)],
            out_specs=tuple(specs),
        ),
        compiler_params=pltpu.CompilerParams(vmem_limit_bytes=VMEM_LIMIT),
        cost_estimate=pl.CostEstimate(
            flops=2 * rows * d * n * count * HD,
            bytes_accessed=2 * (rows * d + n * d * count * HD + n * rows * count * HD),
            transcendentals=0,
        ),
    )(table, tokens, gq, gk, after, *([weight] * (n * pair)))
    return out if near_count else out[0]


def attend_rows(queries, keys, values, factor):
    scores = lax.dot_general(
        queries, keys, (((1,), (1,)), ((), ())), preferred_element_type=jnp.float32
    )
    weight = jnp.exp2(scores * factor).astype(jnp.bfloat16)
    both = jnp.dot(weight, values, preferred_element_type=jnp.float32)
    return (both[:, :HD] / both[:, HD:]).astype(jnp.bfloat16)


def space_attend_kernel(factor, parts, side, q_ref, kv_ref, prev_ref, next_ref, bias_ref, after_ref, out_ref, ka, va, marks):
    rows = q_ref.shape[0]
    near = prev_ref.shape[1]
    total = rows + 2 * near

    @pl.when(pl.program_id(0) == 0)
    def _():
        va[:, HD:] = jnp.ones((total, HD), jnp.bfloat16)
        row = lax.broadcasted_iota(jnp.int32, (rows, HD), 0) // BLOCK
        lane = lax.broadcasted_iota(jnp.int32, (rows, HD), 1)
        marks[...] = jnp.where(row == lane, 1.0, 0.0).astype(jnp.bfloat16)

    for slot, ref in ((0, ka), (1, va)):
        ref[:rows, :HD] = kv_ref[slot]
        ref[rows : rows + near, :HD] = prev_ref[slot]
        ref[rows + near :, :HD] = next_ref[slot]
    for b in range(total // BLOCK):
        ka[b * BLOCK : (b + 1) * BLOCK, HD:] = jnp.broadcast_to(
            bias_ref[b : b + 1, :], (BLOCK, HD)
        ).astype(jnp.bfloat16)
    part = rows // parts
    step = chunk_rows(part, 256)
    for m in range(rows // step):
        span = slice(m * step, (m + 1) * step)
        queries = jnp.concatenate([q_ref[span, :], marks[span, :]], axis=1)
        result = attend_rows(queries, ka[...], va[...], factor)
        which = lax.rem(m * step // part - side[0] + parts, parts)
        first = m * step % part
        out_ref[which, first : first + step, :] = result


def space_attend(q, kv, prev_kv, next_kv, bias, parts, side, after):
    count = q.shape[1]
    rows = q.shape[2]
    near = prev_kv.shape[2]
    total = rows + 2 * near
    factor = math.log2(math.e) / math.sqrt(HD)
    near_spec = pl.BlockSpec((2, None, near, HD), lambda h, t: (0, h, 0, 0))
    part = rows // parts
    return pl.pallas_call(
        functools.partial(space_attend_kernel, factor, parts),
        out_shape=jax.ShapeDtypeStruct((parts, count, part, HD), jnp.bfloat16),
        grid_spec=pltpu.PrefetchScalarGridSpec(
            num_scalar_prefetch=1,
            grid=(count,),
            in_specs=[
                pl.BlockSpec((None, None, rows, HD), lambda h, t: (0, h, 0, 0)),
                pl.BlockSpec((2, None, rows, HD), lambda h, t: (0, h, 0, 0)),
                near_spec,
                near_spec,
                pl.BlockSpec((None, total // BLOCK, HD), lambda h, t: (h, 0, 0)),
                pl.BlockSpec(memory_space=pl.ANY),
            ],
            out_specs=pl.BlockSpec((parts, None, part, HD), lambda h, t: (0, h, 0, 0)),
            scratch_shapes=[
                pltpu.VMEM((total, 2 * HD), jnp.bfloat16),
                pltpu.VMEM((total, 2 * HD), jnp.bfloat16),
                pltpu.VMEM((rows, HD), jnp.bfloat16),
            ],
        ),
        compiler_params=pltpu.CompilerParams(vmem_limit_bytes=VMEM_LIMIT),
        cost_estimate=pl.CostEstimate(
            flops=8 * count * rows * total * HD,
            bytes_accessed=2 * HD * count * (4 * rows + 4 * near),
            transcendentals=count * rows * total,
        ),
        name="space_attend",
    )(side, q, kv, prev_kv, next_kv, bias, after)


def time_attend_kernel(factor, blocks, mask, x_ref, after_ref, out_ref, ka, va):
    frames, _, pos, _ = x_ref.shape
    rows = frames * pos
    span = pos * (BLOCK // STRIP)
    head = pl.program_id(0)
    ka[:, :HD] = x_ref[:, 1].reshape(rows, HD)
    va[:, :HD] = x_ref[:, 2].reshape(rows, HD)
    va[:, HD:] = jnp.ones((rows, HD), jnp.bfloat16)
    row = lax.broadcasted_iota(jnp.int32, (rows, HD), 0)
    lane = lax.broadcasted_iota(jnp.int32, (rows, HD), 1)
    strip = lax.rem(row, pos) // STRIP
    block = row // span
    lane_strip, lane_block = lane // blocks, lax.rem(lane, blocks)
    live = jnp.zeros((rows, HD), jnp.float32)
    for a in range(blocks):
        for b in range(blocks):
            m = mask[(head * blocks + a) * blocks + b].astype(jnp.float32)
            live = jnp.where((lane_block == a) & (block == b), m, live)
    live = jnp.where(strip == lane_strip, live, 0.0)
    ka[:, HD:] = ((live - 1.0) * BIG).astype(jnp.bfloat16)
    marks = jnp.where(strip * blocks + block == lane, 1.0, 0.0).astype(jnp.bfloat16)
    queries = jnp.concatenate([x_ref[:, 0].reshape(rows, HD), marks], axis=1)
    step = chunk_rows(rows, 256)
    per = step // pos
    parts, q = out_ref.shape[1], out_ref.shape[2]
    for m in range(rows // step):
        result = attend_rows(queries[m * step : (m + 1) * step], ka[...], va[...], factor)
        out_ref[m * per : (m + 1) * per] = result.reshape(per, parts, q, HD)


def time_attend(received, mask, after, deal):
    frames, _, count, pos, _ = received.shape
    rows = frames * pos
    factor = math.log2(math.e) / math.sqrt(HD)
    return pl.pallas_call(
        functools.partial(time_attend_kernel, factor, mask.shape[1]),
        out_shape=jax.ShapeDtypeStruct((frames, deal, count, pos // deal, HD), jnp.bfloat16),
        grid_spec=pltpu.PrefetchScalarGridSpec(
            num_scalar_prefetch=1,
            grid=(count,),
            in_specs=[
                pl.BlockSpec((frames, 3, None, pos, HD), lambda h, t: (0, 0, h, 0, 0)),
                pl.BlockSpec(memory_space=pl.ANY),
            ],
            out_specs=pl.BlockSpec((frames, deal, None, pos // deal, HD), lambda h, t: (0, 0, h, 0, 0)),
            scratch_shapes=[
                pltpu.VMEM((rows, 2 * HD), jnp.bfloat16),
                pltpu.VMEM((rows, 2 * HD), jnp.bfloat16),
            ],
        ),
        compiler_params=pltpu.CompilerParams(vmem_limit_bytes=VMEM_LIMIT),
        cost_estimate=pl.CostEstimate(
            flops=8 * count * rows * rows * HD,
            bytes_accessed=8 * HD * count * rows,
            transcendentals=count * rows * rows,
        ),
        name="time_attend",
    )(mask.reshape(-1), received, after)


def place_space_kernel(sources, table, *refs):
    h = pl.program_id(0)
    chosen = table[pl.num_programs(0) + h]
    out_ref = refs[-1]
    for n in range(sources):

        @pl.when(chosen == n)
        def _():
            out_ref[...] = refs[n][...]


def place_space(columns, chosen, sources, width):
    count = columns.shape[0]
    rows = sources[0][0].shape[1]

    def spec(n):
        return pl.BlockSpec((None, rows, HD), lambda h, t: (t[(2 + n) * count + h], 0, 0))

    return pl.pallas_call(
        functools.partial(place_space_kernel, len(sources)),
        out_shape=jax.ShapeDtypeStruct((rows, width), jnp.bfloat16),
        grid_spec=pltpu.PrefetchScalarGridSpec(
            num_scalar_prefetch=1,
            grid=(count,),
            in_specs=[spec(n) for n in range(len(sources))],
            out_specs=pl.BlockSpec((rows, HD), lambda h, t: (0, t[h])),
        ),
        cost_estimate=pl.CostEstimate(flops=0, bytes_accessed=4 * rows * count * HD, transcendentals=0),
        name="place_space",
    )(jnp.concatenate([columns, chosen] + [at for _, at in sources]), *[array for array, _ in sources])


def place_time_kernel(pick, count, table, timed_ref, placed_ref, out_ref, held, sems):
    copies = []
    for g in range(count):
        held[g] = pick(timed_ref, g).reshape(held.shape[1:])
        column = pl.ds(pl.multiple_of(table[g] * HD, HD), HD)
        copies.append(pltpu.make_async_copy(held.at[g], out_ref.at[:, column], sems.at[g]))
        copies[-1].start()
    for copy in copies:
        copy.wait()


def place_time(columns, timed, pick, placed):
    rows = placed.shape[0]
    count = columns.shape[0]
    return pl.pallas_call(
        functools.partial(place_time_kernel, pick, count),
        out_shape=jax.ShapeDtypeStruct(placed.shape, placed.dtype),
        grid_spec=pltpu.PrefetchScalarGridSpec(
            num_scalar_prefetch=1,
            grid=(1,),
            in_specs=[
                pl.BlockSpec(memory_space=pltpu.VMEM),
                pl.BlockSpec(memory_space=pl.ANY),
            ],
            out_specs=pl.BlockSpec(memory_space=pl.ANY),
            scratch_shapes=[
                pltpu.VMEM((count, rows, HD), jnp.bfloat16),
                pltpu.SemaphoreType.DMA((count,)),
            ],
        ),
        input_output_aliases={2: 0},
        compiler_params=pltpu.CompilerParams(vmem_limit_bytes=16 * 1024 * 1024),
        cost_estimate=pl.CostEstimate(
            flops=0, bytes_accessed=4 * rows * count * HD, transcendentals=0
        ),
        name="place_time",
    )(columns, timed, placed)


MESH = pl.DeviceIdType.MESH
FUSED_VMEM = 67_043_328


def spread(i, count):
    return count // 2 + ((i + 1) // 2) * (2 * lax.rem(i, 2) - 1)


def fused_kernel(
    factor,
    blocks,
    table,
    bias_ref,
    gq_ref,
    gk_ref,
    x_hbm,
    w_hbm,
    slots_hbm,
    own_hbm,
    other_hbm,
    back_hbm,
    their_hbm,
    x_v,
    w0k,
    w0v,
    w0q,
    w1k,
    w1v,
    w1q,
    tsend,
    trecv,
    kv,
    nsend,
    nrecv,
    qv,
    ka,
    va,
    marks,
    sout,
    tout,
    x_sem,
    w_sem,
    t_send,
    t_recv,
    n_send,
    n_recv,
    s_send,
    s_recv,
    o_sem,
    r_send,
    r_recv,
    l_send,
    l_recv,
):
    frames = lax.axis_size("frame")
    sides = lax.axis_size("head")
    me_f = lax.axis_index("frame")
    me_s = lax.axis_index("head")
    devices = frames * sides
    me = me_f * sides + me_s
    rows, _ = x_v.shape
    held = (((w0q, w0k, w0v), (w1q, w1k, w1v)))
    half = w0k.shape[0]
    groups = 2 * half
    pairs = groups // 2
    pos = tsend.shape[4]
    q = pos // sides
    slots_near = nsend.shape[4]
    near = slots_near * BLOCK
    total = ka.shape[0]
    step = rows // sides
    picks_at = 3 * groups
    mask_at = picks_at + groups * 2 * 2 * slots_near

    def x_copy(m):
        span = pl.ds(m * step, step)
        return pltpu.make_async_copy(x_hbm.at[span], x_v.at[span], x_sem.at[m])

    class Weights:
        def __init__(self, kind, g):
            self.parts = [
                pltpu.make_async_copy(
                    w_hbm.at[kind, :, pl.ds((3 * g + t) * HD, HD)], held[g // half][kind].at[g % half, t], w_sem.at[kind, g, t]
                )
                for t in range(3)
            ]

        def start(self):
            for copy in self.parts:
                copy.start()

        def wait(self):
            for copy in self.parts:
                copy.wait()

    w_copy = Weights

    order = [(kind, p * half + j) for p in range(2) for kind in (1, 2, 0) for j in range(half)]
    x_copy(0).start()
    for n, (kind, g) in enumerate(order):
        w_copy(kind, g).start()
        if n == 1:
            for m in range(1, sides):
                x_copy(m).start()

    barrier = pltpu.get_barrier_semaphore()

    def greet(i, c):
        other = lax.rem(me + i, devices)
        pl.semaphore_signal(
            barrier, inc=1, device_id={"frame": other // sides, "head": lax.rem(other, sides)}, device_id_type=MESH
        )
        return c

    lax.fori_loop(1, devices, greet, 0)

    row = lax.broadcasted_iota(jnp.int32, (rows, HD), 0)
    lane = lax.broadcasted_iota(jnp.int32, (rows, HD), 1)
    marks[...] = jnp.where(row // BLOCK == lane, 1.0, 0.0).astype(jnp.bfloat16)
    va[:, HD:] = jnp.ones((total, HD), jnp.bfloat16)
    gains = {0: gq_ref[...], 1: gk_ref[...]}

    @pl.when(me_f == 0)
    def _():
        nrecv[0] = jnp.zeros(nrecv.shape[1:], nrecv.dtype)

    @pl.when(me_f == frames - 1)
    def _():
        nrecv[1] = jnp.zeros(nrecv.shape[1:], nrecv.dtype)

    pl.semaphore_wait(barrier, devices - 1)
    labels_copy = pltpu.make_async_remote_copy(
        src_ref=slots_hbm,
        dst_ref=their_hbm,
        send_sem=l_send,
        recv_sem=l_recv,
        device_id={"frame": me_f, "head": 1 - me_s},
        device_id_type=MESH,
    )
    labels_copy.start()

    def time_slot(g):
        return table[g]

    def first_slot(g):
        return table[groups + g]

    def second_slot(g):
        return table[2 * groups + g]

    def weight(kind, p, g, slot):
        return held[p][kind][g - p * half, slot]

    def project_pair(kind, p, first, second, store, wait_x=False):
        def body(m, c):
            if wait_x:
                x_copy(m).wait()
            x = x_v[pl.ds(pl.multiple_of(m * step, step), step), :]
            w = jnp.concatenate([weight(kind, p, *first), weight(kind, p, *second)], axis=1)
            product = jnp.dot(x, w, preferred_element_type=jnp.float32)
            for j in range(2):
                part = product[:, j * HD : (j + 1) * HD]
                if kind in gains:
                    part = normed_head(part, gains[kind])
                else:
                    part = part.astype(jnp.bfloat16)
                store(m, j, part)
            return c

        lax.fori_loop(0, rows // step, body, 0)

    def time_project(p, wait_x):
        ga, gb = 2 * p, 2 * p + 1
        for n, kind in enumerate((1, 2, 0)):
            w_copy(kind, ga).wait()
            w_copy(kind, gb).wait()

            def store(m, j, part, kind=kind):
                at = pl.ds(pl.multiple_of(m * q, q), q)
                tsend[p, kind, :, j, at, :] = part.reshape(frames, q, HD)

            project_pair(kind, p, (ga, time_slot(ga)), (gb, time_slot(gb)), store, wait_x and n == 0)
            pltpu.make_async_copy(tsend.at[p, kind, me_f], trecv.at[p, kind, me_f], t_recv.at[p, kind]).start()

            def send(i, c, kind=kind):
                to = lax.rem(me_f + spread(i, frames), frames)
                pltpu.make_async_remote_copy(
                    src_ref=tsend.at[p, kind, to],
                    dst_ref=trecv.at[p, kind, me_f],
                    send_sem=t_send.at[p, kind],
                    recv_sem=t_recv.at[p, kind],
                    device_id={"frame": to, "head": me_s},
                    device_id_type=MESH,
                ).start()
                return c

            lax.fori_loop(0, frames - 1, send, 0)

    def near_copy(side, g):
        to = me_f + 1 if side == 0 else me_f - 1
        return pltpu.make_async_remote_copy(
            src_ref=nsend.at[side, g],
            dst_ref=nrecv.at[side, g],
            send_sem=n_send.at[side, g],
            recv_sem=n_recv.at[side, g],
            device_id={"frame": to, "head": me_s},
            device_id_type=MESH,
        )

    def space_project(p, g, c):
        for kind in (1, 2):

            def store(m, j, part, kind=kind):
                per = step // BLOCK
                kv[kind - 1, 2 * g + j, pl.ds(m * per, per)] = part.reshape(per, BLOCK, HD)

            project_pair(kind, p, (g, first_slot(g)), (g, second_slot(g)), store)
        for side in range(2):
            for j in range(2):
                for s in range(slots_near):
                    b = table[picks_at + ((2 * g + j) * 2 + side) * slots_near + s]
                    for n in range(2):
                        nsend[side, g, n, j, s] = kv[n, 2 * g + j, b]

        @pl.when(me_f < frames - 1)
        def _():
            near_copy(0, g).start()

        @pl.when(me_f > 0)
        def _():
            near_copy(1, g).start()

        return c

    def own_copy(g):
        span = pl.ds(2 * g, 2)
        return pltpu.make_async_copy(sout.at[0, span], own_hbm.at[span], o_sem.at[g])

    def other_copy(g):
        span = pl.ds(2 * g, 2)
        return pltpu.make_async_remote_copy(
            src_ref=sout.at[1, span],
            dst_ref=other_hbm.at[span],
            send_sem=s_send.at[g],
            recv_sem=s_recv.at[g],
            device_id={"frame": me_f, "head": 1 - me_s},
            device_id_type=MESH,
        )

    def space_mix(p, g, c):
        def store(m, j, part):
            qv[j, pl.ds(pl.multiple_of(m * step, step), step), :] = part

        project_pair(0, p, (g, first_slot(g)), (g, second_slot(g)), store)

        @pl.when(me_f > 0)
        def _():
            near_copy(0, g).wait_recv()

        @pl.when(me_f < frames - 1)
        def _():
            near_copy(1, g).wait_recv()

        def one(j, c):
            h = 2 * g + j
            for n, ref in ((0, ka), (1, va)):
                ref[:rows, :HD] = kv[n, h].reshape(rows, HD)
                ref[rows : rows + near, :HD] = nrecv[0, g, n, j].reshape(near, HD)
                ref[rows + near :, :HD] = nrecv[1, g, n, j].reshape(near, HD)
            for b in range(total // BLOCK):
                ka[b * BLOCK : (b + 1) * BLOCK, HD:] = jnp.broadcast_to(
                    bias_ref[h, b : b + 1, :], (BLOCK, HD)
                ).astype(jnp.bfloat16)
            part = rows // sides
            size = chunk_rows(part, 256)
            for m in range(rows // size):
                span = slice(m * size, (m + 1) * size)
                queries = jnp.concatenate([qv[j, span, :], marks[span, :]], axis=1)
                result = attend_rows(queries, ka[...], va[...], factor)
                which = lax.rem(m * size // part - me_s + sides, sides)
                first = m * size % part
                sout[which, h, first : first + size, :] = result
            return c

        lax.fori_loop(0, 2, one, 0)
        own_copy(g).start()
        other_copy(g).start()
        return c

    def time_mix(p):
        for kind in range(3):
            pltpu.make_async_copy(trecv.at[p, kind], trecv.at[p, kind], t_recv.at[p, kind]).wait()
        span = pos * (BLOCK // STRIP)

        def one(j, c):
            head = 2 * p + j
            ka[:rows, :HD] = trecv[p, 1, :, j].reshape(rows, HD)
            va[:rows, :HD] = trecv[p, 2, :, j].reshape(rows, HD)
            strip = lax.rem(row, pos) // STRIP
            block = row // span
            lane_strip, lane_block = lane // blocks, lax.rem(lane, blocks)
            live = jnp.zeros((rows, HD), jnp.float32)
            for a in range(blocks):
                for b in range(blocks):
                    m = table[mask_at + (head * blocks + a) * blocks + b].astype(jnp.float32)
                    live = jnp.where((lane_block == a) & (block == b), m, live)
            live = jnp.where(strip == lane_strip, live, 0.0)
            ka[:rows, HD:] = ((live - 1.0) * BIG).astype(jnp.bfloat16)
            tags = jnp.where(strip * blocks + block == lane, 1.0, 0.0).astype(jnp.bfloat16)
            queries = jnp.concatenate([trecv[p, 0, :, j].reshape(rows, HD), tags], axis=1)
            size = chunk_rows(rows, 256)
            per = size // pos
            for m in range(rows // size):
                result = attend_rows(queries[m * size : (m + 1) * size], ka[:rows], va[:rows], factor)
                tout[p, m * per * sides : (m + 1) * per * sides, j] = result.reshape(per * sides, q, HD)
            return c

        lax.fori_loop(0, 2, one, 0)
        heads = pl.ds(2 * p, 2)
        pltpu.make_async_copy(tout.at[p, me], back_hbm.at[me_f, me_s, heads], r_recv.at[p]).start()

        def send(i, c):
            to = lax.rem(me + spread(i, devices), devices)
            pltpu.make_async_remote_copy(
                src_ref=tout.at[p, to],
                dst_ref=back_hbm.at[me_f, me_s, heads],
                send_sem=r_send.at[p],
                recv_sem=r_recv.at[p],
                device_id={"frame": to // sides, "head": lax.rem(to, sides)},
                device_id_type=MESH,
            ).start()
            return c

        lax.fori_loop(0, devices - 1, send, 0)

    time_project(0, True)
    for p in range(1, pairs):
        time_project(p, False)
    for p in range(pairs):
        lax.fori_loop(2 * p, 2 * p + 2, functools.partial(space_project, p), 0)
    for p in range(pairs):
        lax.fori_loop(2 * p, 2 * p + 2, functools.partial(space_mix, p), 0)
        time_mix(p)

    def drain(g, c):
        own_copy(g).wait()
        other_copy(g).wait()

        @pl.when(me_f < frames - 1)
        def _():
            near_copy(0, g).wait_send()

        @pl.when(me_f > 0)
        def _():
            near_copy(1, g).wait_send()

        return c

    lax.fori_loop(0, groups, drain, 0)
    for p in range(pairs):
        for kind in range(3):
            sent = tsend.at[p, kind, pl.ds(0, frames - 1)]
            pltpu.make_async_copy(sent, sent, t_send.at[p, kind]).wait()
        sent = tout.at[p, pl.ds(0, devices - 1)]
        pltpu.make_async_copy(sent, sent, r_send.at[p]).wait()
        pltpu.make_async_copy(tout.at[p], tout.at[p], r_recv.at[p]).wait()
    labels_copy.wait()


def fused(tokens, weight, gq, gk, slots, first, second, picks, time_live, bias):
    rows, d = tokens.shape
    frames = lax.axis_size("frame")
    sides = lax.axis_size("head")
    groups = slots.shape[0]
    pairs = groups // 2
    heads = 2 * groups
    near = NEAR_MAX * BLOCK
    total = rows + 2 * near
    pos = rows // frames
    q = pos // sides
    part = rows // sides
    blocks = time_live.shape[1]
    table = jnp.concatenate([slots, first, second, picks.reshape(-1), time_live.reshape(-1)])
    slots_row = jnp.pad(slots, (0, HD - groups)).reshape(1, HD)
    bf = jnp.bfloat16
    any_spec = pl.BlockSpec(memory_space=pl.ANY)
    vmem_spec = pl.BlockSpec(memory_space=pltpu.VMEM)
    dma = pltpu.SemaphoreType.DMA
    return pl.pallas_call(
        functools.partial(fused_kernel, math.log2(math.e) / math.sqrt(HD), blocks),
        out_shape=(
            jax.ShapeDtypeStruct((heads, part, HD), bf),
            jax.ShapeDtypeStruct((heads, part, HD), bf),
            jax.ShapeDtypeStruct((frames, sides, groups, q, HD), bf),
            jax.ShapeDtypeStruct((1, HD), jnp.int32),
        ),
        in_specs=[pl.BlockSpec(memory_space=pltpu.SMEM), vmem_spec, vmem_spec, vmem_spec, any_spec, any_spec, any_spec],
        out_specs=(any_spec,) * 4,
        scratch_shapes=[
            pltpu.VMEM((rows, d), bf),
        ]
        + [pltpu.VMEM((groups // 2, 3, d, HD), bf)] * 6
        + [
            pltpu.VMEM((pairs, 3, frames, 2, pos, HD), bf),
            pltpu.VMEM((pairs, 3, frames, 2, pos, HD), bf),
            pltpu.VMEM((2, heads, rows // BLOCK, BLOCK, HD), bf),
            pltpu.VMEM((2, groups, 2, 2, NEAR_MAX, BLOCK, HD), bf),
            pltpu.VMEM((2, groups, 2, 2, NEAR_MAX, BLOCK, HD), bf),
            pltpu.VMEM((2, rows, HD), bf),
            pltpu.VMEM((total, 2 * HD), bf),
            pltpu.VMEM((total, 2 * HD), bf),
            pltpu.VMEM((rows, HD), bf),
            pltpu.VMEM((sides, heads, part, HD), bf),
            pltpu.VMEM((pairs, frames * sides, 2, q, HD), bf),
            dma((sides,)),
            dma((3, groups, 3)),
            dma((pairs, 3)),
            dma((pairs, 3)),
            dma((2, groups)),
            dma((2, groups)),
            dma((groups,)),
            dma((groups,)),
            dma((groups,)),
            dma((pairs,)),
            dma((pairs,)),
            dma,
            dma,
        ],
        compiler_params=pltpu.CompilerParams(
            vmem_limit_bytes=FUSED_VMEM, collective_id=0, has_side_effects=True
        ),
        name="fused",
    )(table, bias, gq, gk, tokens, weight, slots_row)


def place_kernel(mine_ref, theirs_ref, own_ref, other_ref, back_ref, out_ref):
    side = lax.axis_index("head")
    groups = back_ref.shape[2]
    rows = out_ref.shape[0]

    def put(head, value):
        out_ref[:, pl.ds(pl.multiple_of(head * HD, HD), HD)] = value

    for g in range(groups):
        for whose, slots, ref in ((side, mine_ref, own_ref), (1 - side, theirs_ref, other_ref)):
            slot = slots[0, g]
            base = 3 * (whose * groups + g)
            put(base + jnp.where(slot == 0, 1, 0), ref[2 * g])
            put(base + jnp.where(slot == 2, 1, 2), ref[2 * g + 1])
            put(base + slot, back_ref[:, whose, g].reshape(rows, HD))


def place(mine, theirs, own, other, back):
    heads, rows, _ = own.shape
    _, sides, groups, q, _ = back.shape
    size = chunk_rows(rows, 128)
    scalar = pl.BlockSpec(memory_space=pltpu.SMEM)
    space = pl.BlockSpec((heads, size, HD), lambda i: (0, i, 0))
    return pl.pallas_call(
        place_kernel,
        out_shape=jax.ShapeDtypeStruct((rows, sides * groups * 3 * HD), jnp.bfloat16),
        grid=(rows // size,),
        in_specs=[
            scalar,
            scalar,
            space,
            space,
            pl.BlockSpec((size // q, sides, groups, q, HD), lambda i: (i, 0, 0, 0, 0)),
        ],
        out_specs=pl.BlockSpec((size, sides * groups * 3 * HD), lambda i: (i, 0)),
        name="place",
    )(mine, theirs, own, other, back)


def block_picks(live):
    used = jnp.max(live, axis=1)
    width = used.shape[1]
    before = (jnp.arange(width)[:, None] < jnp.arange(width)[None, :]).astype(jnp.int32)
    rank = jnp.sum(used[:, :, None] * before[None], axis=1)
    return used[:, None, :] * (rank[:, None, :] == jnp.arange(NEAR_MAX)[None, :, None]).astype(jnp.int32)


def on_device(tokens, qkv_weight, query_gain, key_gain, labels, space_mask, time_mask):
    frame_count = lax.axis_size("frame")
    sides = lax.axis_size("head")
    own_frame = lax.axis_index("frame")
    own_side = lax.axis_index("head")
    row_count = tokens.shape[0]
    groups = labels.shape[0] // 3
    blocks = row_count // BLOCK
    space_count = 2 * groups
    gq, gk = query_gain.reshape(1, HD), key_gain.reshape(1, HD)

    picked = labels.reshape(groups, 3)
    time_slot = jnp.sum(picked * jnp.arange(3, dtype=jnp.int32)[None, :], axis=1)
    group_base = 3 * jnp.arange(groups, dtype=jnp.int32)
    time_heads = group_base + time_slot
    first_space = group_base + jnp.where(time_slot == 0, 1, 0)
    second_space = group_base + jnp.where(time_slot == 2, 1, 2)
    space_heads = jnp.stack([first_space, second_space], axis=1).reshape(space_count)

    live = jnp.take(space_mask, space_heads, axis=0)
    low, own, high = live[:, :, :blocks], live[:, :, blocks : 2 * blocks], live[:, :, 2 * blocks :]
    low_pick, high_pick = block_picks(low), block_picks(high)
    ids = jnp.arange(blocks, dtype=jnp.int32)
    picks = jnp.stack([jnp.sum(low_pick * ids, axis=-1), jnp.sum(high_pick * ids, axis=-1)], axis=1)
    low_ok = (own_frame > 0).astype(jnp.int32)
    high_ok = (own_frame < frame_count - 1).astype(jnp.int32)

    def near_live(pick, side, ok):
        return ok * jnp.sum(pick[:, :, None, :] * side[:, None, :, :], axis=-1)

    allowed = jnp.concatenate(
        [jnp.swapaxes(own, 1, 2), near_live(low_pick, low, low_ok), near_live(high_pick, high, high_ok)],
        axis=1,
    )
    bias = jnp.pad((allowed.astype(jnp.float32) - 1.0) * BIG, ((0, 0), (0, 0), (0, HD - blocks)))

    pos_count = row_count // frame_count
    deal = sides if pos_count % (sides * STRIP) == 0 else 1
    if sides == 2 and deal == 2 and groups == 4:
        mask = jnp.take(time_mask, time_heads, axis=0)
        own_out, other_out, back, theirs = fused(
            tokens, qkv_weight, gq, gk, time_slot, first_space - group_base, second_space - group_base, picks, mask, bias
        )
        mine = jnp.pad(time_slot, (0, HD - groups)).reshape(1, HD)
        return place(mine, theirs, own_out, other_out, back)
    up = [(i, i + 1) for i in range(frame_count - 1)]
    down = [(i + 1, i) for i in range(frame_count - 1)]
    swap = [(0, 1), (1, 0)]
    kv, to_next, to_prev = project(tokens, qkv_weight, gq, gk, space_heads, (1, 2), gq, picks=picks)
    prev_kv = lax.ppermute(to_next, "frame", up)
    next_kv = lax.ppermute(to_prev, "frame", down)
    packed = project(
        tokens, qkv_weight, gq, gk, time_heads, (0, 1, 2), kv, strips=frame_count, deal=deal
    )
    received = lax.all_to_all(packed, "frame", split_axis=0, concat_axis=0, tiled=True)
    query_heads = space_heads
    if sides == 2:
        their_slot = lax.ppermute(time_slot, "head", swap)
        query_heads, their_slot = lax.optimization_barrier((space_heads, their_slot))
        slots = jnp.where(
            own_side == 0,
            jnp.concatenate([time_slot, their_slot]),
            jnp.concatenate([their_slot, time_slot]),
        )
    else:
        slots = lax.all_to_all(
            jnp.broadcast_to(time_slot[None], (sides, groups)), "head", 0, 0, tiled=True
        ).reshape(-1)
    space_q = project(tokens, qkv_weight, gq, gk, query_heads, (0,), packed)

    side = jnp.reshape(own_side if sides == 2 else jnp.int32(0), (1,)).astype(jnp.int32)
    space_out = space_attend(space_q, kv, prev_kv, next_kv, bias, sides, side, space_q)
    mask = jnp.take(time_mask, time_heads, axis=0)
    time_out = time_attend(received, mask, space_out, deal)

    part_rows = row_count // sides
    total_heads = sides * space_count
    head_ids = jnp.arange(total_heads, dtype=jnp.int32)
    if sides == 2:
        space_recv = lax.ppermute(space_out[1], "head", swap)

        def clamped(whose):
            return jnp.clip(head_ids - whose * space_count, 0, space_count - 1)

        sources = [(space_out[0], clamped(own_side)), (space_recv, clamped(1 - own_side))]
        chosen = (head_ids // space_count != own_side).astype(jnp.int32)
    else:
        space_all = lax.all_to_all(space_out, "head", 0, 0, tiled=True)
        sources = [(space_all.reshape(total_heads, part_rows, HD), head_ids)]
        chosen = jnp.zeros_like(head_ids)
    all_groups = jnp.arange(sides * groups, dtype=jnp.int32)
    firsts = 3 * all_groups + jnp.where(slots == 0, 1, 0)
    seconds = 3 * all_groups + jnp.where(slots == 2, 1, 2)
    space_columns = jnp.stack([firsts, seconds], axis=1).reshape(total_heads)
    placed = place_space(space_columns, chosen, sources, sides * groups * 3 * HD)

    if deal == sides:
        q = pos_count // sides
        timed = lax.all_to_all(
            time_out.reshape(frame_count * sides, groups, q, HD), ("frame", "head"), 0, 0, tiled=True
        )
        timed = timed.reshape(frame_count, sides, groups, q, HD)

        def pick(ref, g):
            return ref[:, g // groups, g % groups]

    else:
        timed = time_out.reshape(frame_count, groups, pos_count, HD)
        timed = lax.all_to_all(timed, "frame", 0, 0, tiled=True)
        timed = lax.all_to_all(timed, "head", 0, 0, tiled=True)
        timed = timed.reshape(sides, frame_count // sides, groups, pos_count, HD)

        def pick(ref, g):
            return ref[g // groups, :, g % groups]

    return place_time(3 * all_groups + slots, timed, pick, placed)


def solution(mesh):
    placed = (
        P("frame", None),
        P(None, None, "head"),
        P(),
        P(),
        P("head"),
        P("head", None, None),
        P("head", None, None),
    )

    return jax.shard_map(
        on_device, mesh=mesh, in_specs=placed, out_specs=P(("frame", "head"), None), check_vma=False
    )
```

```python
import functools
import math

import jax
import jax.numpy as jnp
from jax import lax
from jax.experimental import pallas as pl
from jax.experimental.pallas import tpu as pltpu
from jax.sharding import PartitionSpec as P


STRIP = 8
BLOCK = 64
NEAR_MAX = 8
HD = 128
epsilon = 1e-06
BIG = 1e30
VMEM_LIMIT = 56 * 1024 * 1024


def chunk_rows(rows, want):
    while rows % want:
        want //= 2
    return want


def normed_head(projected, gains):
    inverse_rms = lax.rsqrt(jnp.mean(projected * projected, axis=-1, keepdims=True) + epsilon)
    return (projected * inverse_rms * gains).astype(jnp.bfloat16)


def project_kernel(kinds, pair, near_count, strips, table, x_ref, gq_ref, gk_ref, after_ref, *refs):
    weights = refs[: len(kinds) * pair]
    outs = refs[len(kinds) * pair :]
    out_ref = outs[0]
    i = pl.program_id(0)
    count = pl.num_programs(0) * pair
    step = x_ref.shape[0] // strips if strips > 1 else chunk_rows(x_ref.shape[0], 512)
    gains = {0: gq_ref[...], 1: gk_ref[...]}

    def body(m, carry):
        rows = pl.ds(pl.multiple_of(m * step, step), step)
        x = x_ref[rows, :]
        for n, kind in enumerate(kinds):
            w = [w_ref[...] for w_ref in weights[n * pair : (n + 1) * pair]]
            w = w[0] if pair == 1 else jnp.concatenate(w, axis=1)
            product = jnp.dot(x, w, preferred_element_type=jnp.float32)
            for j in range(pair):
                part = product[:, j * HD : (j + 1) * HD]
                if kind in gains:
                    part = normed_head(part, gains[kind])
                else:
                    part = part.astype(jnp.bfloat16)
                if strips:
                    pos = out_ref.shape[3]
                    if strips == 1:
                        per = step // pos
                        out_ref[pl.ds(m * per, per), n, j] = part.reshape(per, pos, HD)
                    else:
                        q = pos // strips
                        at = pl.ds(pl.multiple_of(m * q, q), q)
                        out_ref[:, n, j, at, :] = part.reshape(out_ref.shape[0], q, HD)
                else:
                    out_ref[n, j, rows, :] = part
        return carry

    lax.fori_loop(0, x_ref.shape[0] // step, body, 0)
    for j in range(pair if near_count else 0):
        head = i * pair + j
        for s in range(near_count):
            for side, ref in ((0, outs[1]), (1, outs[2])):
                b = table[count + (head * 2 + side) * near_count + s]
                src = pl.ds(pl.multiple_of(b * BLOCK, BLOCK), BLOCK)
                for n in range(2):
                    ref[n, j, s * BLOCK : (s + 1) * BLOCK, :] = out_ref[n, j, src, :]


def project(tokens, weight, gq, gk, heads, kinds, after, strips=0, deal=1, picks=None):
    rows, d = tokens.shape
    count = heads.shape[0]
    pair = 2 if count % 2 == 0 else 1
    n = len(kinds)
    near_count = 0 if picks is None else NEAR_MAX
    table = heads if picks is None else jnp.concatenate([heads, picks.reshape(-1)])

    def w_spec(kind, j):
        return pl.BlockSpec((None, d, HD), lambda i, t: (kind, 0, t[pair * i + j]))

    gain = pl.BlockSpec((1, HD), lambda i, t: (0, 0))
    if strips:
        pos = rows // strips
        shapes = [jax.ShapeDtypeStruct((strips, n, count, pos, HD), jnp.bfloat16)]
        specs = [pl.BlockSpec((strips, n, pair, pos, HD), lambda i, t: (0, 0, i, 0, 0))]
    else:
        shapes = [jax.ShapeDtypeStruct((n, count, rows, HD), jnp.bfloat16)]
        specs = [pl.BlockSpec((n, pair, rows, HD), lambda i, t: (0, i, 0, 0))]
    if near_count:
        near = near_count * BLOCK
        shapes += [jax.ShapeDtypeStruct((2, count, near, HD), jnp.bfloat16)] * 2
        specs += [pl.BlockSpec((2, pair, near, HD), lambda i, t: (0, i, 0, 0))] * 2
    out = pl.pallas_call(
        functools.partial(project_kernel, kinds, pair, near_count, deal if strips else 0),
        out_shape=tuple(shapes),
        grid_spec=pltpu.PrefetchScalarGridSpec(
            num_scalar_prefetch=1,
            grid=(count // pair,),
            in_specs=[
                pl.BlockSpec((rows, d), lambda i, t: (0, 0), pipeline_mode=pl.Buffered(1)),
                gain,
                gain,
                pl.BlockSpec(memory_space=pl.ANY),
            ]
            + [w_spec(kind, j) for kind in kinds for j in range(pair)],
            out_specs=tuple(specs),
        ),
        compiler_params=pltpu.CompilerParams(vmem_limit_bytes=VMEM_LIMIT),
        cost_estimate=pl.CostEstimate(
            flops=2 * rows * d * n * count * HD,
            bytes_accessed=2 * (rows * d + n * d * count * HD + n * rows * count * HD),
            transcendentals=0,
        ),
    )(table, tokens, gq, gk, after, *([weight] * (n * pair)))
    return out if near_count else out[0]


def attend_rows(queries, keys, values, factor):
    scores = lax.dot_general(
        queries, keys, (((1,), (1,)), ((), ())), preferred_element_type=jnp.float32
    )
    weight = jnp.exp2(scores * factor).astype(jnp.bfloat16)
    both = jnp.dot(weight, values, preferred_element_type=jnp.float32)
    return (both[:, :HD] / both[:, HD:]).astype(jnp.bfloat16)


def space_attend_kernel(factor, parts, side, q_ref, kv_ref, prev_ref, next_ref, bias_ref, after_ref, out_ref, ka, va, marks):
    rows = q_ref.shape[0]
    near = prev_ref.shape[1]
    total = rows + 2 * near

    @pl.when(pl.program_id(0) == 0)
    def _():
        va[:, HD:] = jnp.ones((total, HD), jnp.bfloat16)
        row = lax.broadcasted_iota(jnp.int32, (rows, HD), 0) // BLOCK
        lane = lax.broadcasted_iota(jnp.int32, (rows, HD), 1)
        marks[...] = jnp.where(row == lane, 1.0, 0.0).astype(jnp.bfloat16)

    for slot, ref in ((0, ka), (1, va)):
        ref[:rows, :HD] = kv_ref[slot]
        ref[rows : rows + near, :HD] = prev_ref[slot]
        ref[rows + near :, :HD] = next_ref[slot]
    for b in range(total // BLOCK):
        ka[b * BLOCK : (b + 1) * BLOCK, HD:] = jnp.broadcast_to(
            bias_ref[b : b + 1, :], (BLOCK, HD)
        ).astype(jnp.bfloat16)
    part = rows // parts
    step = chunk_rows(part, 256)
    for m in range(rows // step):
        span = slice(m * step, (m + 1) * step)
        queries = jnp.concatenate([q_ref[span, :], marks[span, :]], axis=1)
        result = attend_rows(queries, ka[...], va[...], factor)
        which = lax.rem(m * step // part - side[0] + parts, parts)
        first = m * step % part
        out_ref[which, first : first + step, :] = result


def space_attend(q, kv, prev_kv, next_kv, bias, parts, side, after):
    count = q.shape[1]
    rows = q.shape[2]
    near = prev_kv.shape[2]
    total = rows + 2 * near
    factor = math.log2(math.e) / math.sqrt(HD)
    near_spec = pl.BlockSpec((2, None, near, HD), lambda h, t: (0, h, 0, 0))
    part = rows // parts
    return pl.pallas_call(
        functools.partial(space_attend_kernel, factor, parts),
        out_shape=jax.ShapeDtypeStruct((parts, count, part, HD), jnp.bfloat16),
        grid_spec=pltpu.PrefetchScalarGridSpec(
            num_scalar_prefetch=1,
            grid=(count,),
            in_specs=[
                pl.BlockSpec((None, None, rows, HD), lambda h, t: (0, h, 0, 0)),
                pl.BlockSpec((2, None, rows, HD), lambda h, t: (0, h, 0, 0)),
                near_spec,
                near_spec,
                pl.BlockSpec((None, total // BLOCK, HD), lambda h, t: (h, 0, 0)),
                pl.BlockSpec(memory_space=pl.ANY),
            ],
            out_specs=pl.BlockSpec((parts, None, part, HD), lambda h, t: (0, h, 0, 0)),
            scratch_shapes=[
                pltpu.VMEM((total, 2 * HD), jnp.bfloat16),
                pltpu.VMEM((total, 2 * HD), jnp.bfloat16),
                pltpu.VMEM((rows, HD), jnp.bfloat16),
            ],
        ),
        compiler_params=pltpu.CompilerParams(vmem_limit_bytes=VMEM_LIMIT),
        cost_estimate=pl.CostEstimate(
            flops=8 * count * rows * total * HD,
            bytes_accessed=2 * HD * count * (4 * rows + 4 * near),
            transcendentals=count * rows * total,
        ),
        name="space_attend",
    )(side, q, kv, prev_kv, next_kv, bias, after)


def time_attend_kernel(factor, blocks, mask, x_ref, after_ref, out_ref, ka, va):
    frames, _, pos, _ = x_ref.shape
    rows = frames * pos
    span = pos * (BLOCK // STRIP)
    head = pl.program_id(0)
    ka[:, :HD] = x_ref[:, 1].reshape(rows, HD)
    va[:, :HD] = x_ref[:, 2].reshape(rows, HD)
    va[:, HD:] = jnp.ones((rows, HD), jnp.bfloat16)
    row = lax.broadcasted_iota(jnp.int32, (rows, HD), 0)
    lane = lax.broadcasted_iota(jnp.int32, (rows, HD), 1)
    strip = lax.rem(row, pos) // STRIP
    block = row // span
    lane_strip, lane_block = lane // blocks, lax.rem(lane, blocks)
    live = jnp.zeros((rows, HD), jnp.float32)
    for a in range(blocks):
        for b in range(blocks):
            m = mask[(head * blocks + a) * blocks + b].astype(jnp.float32)
            live = jnp.where((lane_block == a) & (block == b), m, live)
    live = jnp.where(strip == lane_strip, live, 0.0)
    ka[:, HD:] = ((live - 1.0) * BIG).astype(jnp.bfloat16)
    marks = jnp.where(strip * blocks + block == lane, 1.0, 0.0).astype(jnp.bfloat16)
    queries = jnp.concatenate([x_ref[:, 0].reshape(rows, HD), marks], axis=1)
    step = chunk_rows(rows, 256)
    per = step // pos
    parts, q = out_ref.shape[1], out_ref.shape[2]
    for m in range(rows // step):
        result = attend_rows(queries[m * step : (m + 1) * step], ka[...], va[...], factor)
        out_ref[m * per : (m + 1) * per] = result.reshape(per, parts, q, HD)


def time_attend(received, mask, after, deal):
    frames, _, count, pos, _ = received.shape
    rows = frames * pos
    factor = math.log2(math.e) / math.sqrt(HD)
    return pl.pallas_call(
        functools.partial(time_attend_kernel, factor, mask.shape[1]),
        out_shape=jax.ShapeDtypeStruct((frames, deal, count, pos // deal, HD), jnp.bfloat16),
        grid_spec=pltpu.PrefetchScalarGridSpec(
            num_scalar_prefetch=1,
            grid=(count,),
            in_specs=[
                pl.BlockSpec((frames, 3, None, pos, HD), lambda h, t: (0, 0, h, 0, 0)),
                pl.BlockSpec(memory_space=pl.ANY),
            ],
            out_specs=pl.BlockSpec((frames, deal, None, pos // deal, HD), lambda h, t: (0, 0, h, 0, 0)),
            scratch_shapes=[
                pltpu.VMEM((rows, 2 * HD), jnp.bfloat16),
                pltpu.VMEM((rows, 2 * HD), jnp.bfloat16),
            ],
        ),
        compiler_params=pltpu.CompilerParams(vmem_limit_bytes=VMEM_LIMIT),
        cost_estimate=pl.CostEstimate(
            flops=8 * count * rows * rows * HD,
            bytes_accessed=8 * HD * count * rows,
            transcendentals=count * rows * rows,
        ),
        name="time_attend",
    )(mask.reshape(-1), received, after)


def place_space_kernel(sources, table, *refs):
    h = pl.program_id(0)
    chosen = table[pl.num_programs(0) + h]
    out_ref = refs[-1]
    for n in range(sources):

        @pl.when(chosen == n)
        def _():
            out_ref[...] = refs[n][...]


def place_space(columns, chosen, sources, width):
    count = columns.shape[0]
    rows = sources[0][0].shape[1]

    def spec(n):
        return pl.BlockSpec((None, rows, HD), lambda h, t: (t[(2 + n) * count + h], 0, 0))

    return pl.pallas_call(
        functools.partial(place_space_kernel, len(sources)),
        out_shape=jax.ShapeDtypeStruct((rows, width), jnp.bfloat16),
        grid_spec=pltpu.PrefetchScalarGridSpec(
            num_scalar_prefetch=1,
            grid=(count,),
            in_specs=[spec(n) for n in range(len(sources))],
            out_specs=pl.BlockSpec((rows, HD), lambda h, t: (0, t[h])),
        ),
        cost_estimate=pl.CostEstimate(flops=0, bytes_accessed=4 * rows * count * HD, transcendentals=0),
        name="place_space",
    )(jnp.concatenate([columns, chosen] + [at for _, at in sources]), *[array for array, _ in sources])


def place_time_kernel(pick, count, table, timed_ref, placed_ref, out_ref, held, sems):
    copies = []
    for g in range(count):
        held[g] = pick(timed_ref, g).reshape(held.shape[1:])
        column = pl.ds(pl.multiple_of(table[g] * HD, HD), HD)
        copies.append(pltpu.make_async_copy(held.at[g], out_ref.at[:, column], sems.at[g]))
        copies[-1].start()
    for copy in copies:
        copy.wait()


def place_time(columns, timed, pick, placed):
    rows = placed.shape[0]
    count = columns.shape[0]
    return pl.pallas_call(
        functools.partial(place_time_kernel, pick, count),
        out_shape=jax.ShapeDtypeStruct(placed.shape, placed.dtype),
        grid_spec=pltpu.PrefetchScalarGridSpec(
            num_scalar_prefetch=1,
            grid=(1,),
            in_specs=[
                pl.BlockSpec(memory_space=pltpu.VMEM),
                pl.BlockSpec(memory_space=pl.ANY),
            ],
            out_specs=pl.BlockSpec(memory_space=pl.ANY),
            scratch_shapes=[
                pltpu.VMEM((count, rows, HD), jnp.bfloat16),
                pltpu.SemaphoreType.DMA((count,)),
            ],
        ),
        input_output_aliases={2: 0},
        compiler_params=pltpu.CompilerParams(vmem_limit_bytes=16 * 1024 * 1024),
        cost_estimate=pl.CostEstimate(
            flops=0, bytes_accessed=4 * rows * count * HD, transcendentals=0
        ),
        name="place_time",
    )(columns, timed, placed)


MESH = pl.DeviceIdType.MESH
FUSED_VMEM = 67_043_328


def spread(i, count):
    return count // 2 + ((i + 1) // 2) * (2 * lax.rem(i, 2) - 1)


def fused_kernel(
    factor,
    blocks,
    table,
    picks_ref,
    bias_ref,
    gq_ref,
    gk_ref,
    x_hbm,
    w_hbm,
    slots_hbm,
    own_hbm,
    other_hbm,
    back_hbm,
    their_hbm,
    x_v,
    w0k,
    w0v,
    w0q,
    w1k,
    w1v,
    w1q,
    tsend,
    trecv,
    kv,
    nsend,
    nrecv,
    qv,
    ka,
    va,
    marks,
    sout,
    tout,
    x_sem,
    w_sem,
    t_send,
    t_recv,
    n_send,
    n_recv,
    s_send,
    s_recv,
    o_sem,
    r_send,
    r_recv,
    l_send,
    l_recv,
):
    frames = lax.axis_size("frame")
    sides = lax.axis_size("head")
    me_f = lax.axis_index("frame")
    me_s = lax.axis_index("head")
    devices = frames * sides
    me = me_f * sides + me_s
    rows, _ = x_v.shape
    held = (((w0q, w0k, w0v), (w1q, w1k, w1v)))
    half = w0k.shape[0]
    groups = 2 * half
    pairs = groups // 2
    pos = tsend.shape[4]
    q = pos // sides
    slots_near = nsend.shape[4]
    near = slots_near * BLOCK
    total = ka.shape[0]
    step = rows // sides
    mask_at = 3 * groups
    own_blocks = rows // BLOCK

    def x_copy(m):
        span = pl.ds(m * step, step)
        return pltpu.make_async_copy(x_hbm.at[span], x_v.at[span], x_sem.at[m])

    class Weights:
        def __init__(self, kind, g):
            self.parts = [
                pltpu.make_async_copy(
                    w_hbm.at[kind, :, pl.ds((3 * g + t) * HD, HD)], held[g // half][kind].at[g % half, t], w_sem.at[kind, g, t]
                )
                for t in range(3)
            ]

        def start(self):
            for copy in self.parts:
                copy.start()

        def wait(self):
            for copy in self.parts:
                copy.wait()

    w_copy = Weights

    order = [(kind, p * half + j) for p in range(2) for kind in (1, 2, 0) for j in range(half)]
    x_copy(0).start()
    for n, (kind, g) in enumerate(order):
        w_copy(kind, g).start()
        if n == 1:
            for m in range(1, sides):
                x_copy(m).start()

    barrier = pltpu.get_barrier_semaphore()

    def greet(i, c):
        other = lax.rem(me + i, devices)
        pl.semaphore_signal(
            barrier, inc=1, device_id={"frame": other // sides, "head": lax.rem(other, sides)}, device_id_type=MESH
        )
        return c

    lax.fori_loop(1, devices, greet, 0)

    row = lax.broadcasted_iota(jnp.int32, (rows, HD), 0)
    lane = lax.broadcasted_iota(jnp.int32, (rows, HD), 1)
    marks[...] = jnp.where(row // BLOCK == lane, 1.0, 0.0).astype(jnp.bfloat16)
    va[:, HD:] = jnp.ones((total, HD), jnp.bfloat16)
    gains = {0: gq_ref[...], 1: gk_ref[...]}

    @pl.when(me_f == 0)
    def _():
        nrecv[0] = jnp.zeros(nrecv.shape[1:], nrecv.dtype)

    @pl.when(me_f == frames - 1)
    def _():
        nrecv[1] = jnp.zeros(nrecv.shape[1:], nrecv.dtype)

    pl.semaphore_wait(barrier, devices - 1)
    labels_copy = pltpu.make_async_remote_copy(
        src_ref=slots_hbm,
        dst_ref=their_hbm,
        send_sem=l_send,
        recv_sem=l_recv,
        device_id={"frame": me_f, "head": 1 - me_s},
        device_id_type=MESH,
    )
    labels_copy.start()

    def time_slot(g):
        return table[g]

    def first_slot(g):
        return table[groups + g]

    def second_slot(g):
        return table[2 * groups + g]

    def weight(kind, p, g, slot):
        return held[p][kind][g - p * half, slot]

    def project_pair(kind, p, first, second, store, wait_x=False):
        def body(m, c):
            if wait_x:
                x_copy(m).wait()
            x = x_v[pl.ds(pl.multiple_of(m * step, step), step), :]
            w = jnp.concatenate([weight(kind, p, *first), weight(kind, p, *second)], axis=1)
            product = jnp.dot(x, w, preferred_element_type=jnp.float32)
            for j in range(2):
                part = product[:, j * HD : (j + 1) * HD]
                if kind in gains:
                    part = normed_head(part, gains[kind])
                else:
                    part = part.astype(jnp.bfloat16)
                store(m, j, part)
            return c

        lax.fori_loop(0, rows // step, body, 0)

    def time_project(p, wait_x):
        ga, gb = 2 * p, 2 * p + 1
        for n, kind in enumerate((1, 2, 0)):
            w_copy(kind, ga).wait()
            w_copy(kind, gb).wait()

            def store(m, j, part, kind=kind):
                at = pl.ds(pl.multiple_of(m * q, q), q)
                tsend[p, kind, :, j, at, :] = part.reshape(frames, q, HD)

            project_pair(kind, p, (ga, time_slot(ga)), (gb, time_slot(gb)), store, wait_x and n == 0)
            pltpu.make_async_copy(tsend.at[p, kind, me_f], trecv.at[p, kind, me_f], t_recv.at[p, kind]).start()

            def send(i, c, kind=kind):
                to = lax.rem(me_f + spread(i, frames), frames)
                pltpu.make_async_remote_copy(
                    src_ref=tsend.at[p, kind, to],
                    dst_ref=trecv.at[p, kind, me_f],
                    send_sem=t_send.at[p, kind],
                    recv_sem=t_recv.at[p, kind],
                    device_id={"frame": to, "head": me_s},
                    device_id_type=MESH,
                ).start()
                return c

            lax.fori_loop(0, frames - 1, send, 0)

    def near_copy(side, g):
        to = me_f + 1 if side == 0 else me_f - 1
        return pltpu.make_async_remote_copy(
            src_ref=nsend.at[side, g],
            dst_ref=nrecv.at[side, g],
            send_sem=n_send.at[side, g],
            recv_sem=n_recv.at[side, g],
            device_id={"frame": to, "head": me_s},
            device_id_type=MESH,
        )

    def space_project(p, g, c):
        for kind in (1, 2):

            def store(m, j, part, kind=kind):
                per = step // BLOCK
                kv[kind - 1, 2 * g + j, pl.ds(m * per, per)] = part.reshape(per, BLOCK, HD)

            project_pair(kind, p, (g, first_slot(g)), (g, second_slot(g)), store)
        for side in range(2):
            for j in range(2):
                for s in range(slots_near):
                    b = picks_ref[2 * g + j, own_blocks + side * slots_near + s]
                    for n in range(2):
                        nsend[side, g, n, j, s] = kv[n, 2 * g + j, b]

        @pl.when(me_f < frames - 1)
        def _():
            near_copy(0, g).start()

        @pl.when(me_f > 0)
        def _():
            near_copy(1, g).start()

        return c

    def own_copy(g):
        span = pl.ds(2 * g, 2)
        return pltpu.make_async_copy(sout.at[0, span], own_hbm.at[span], o_sem.at[g])

    def other_copy(g):
        span = pl.ds(2 * g, 2)
        return pltpu.make_async_remote_copy(
            src_ref=sout.at[1, span],
            dst_ref=other_hbm.at[span],
            send_sem=s_send.at[g],
            recv_sem=s_recv.at[g],
            device_id={"frame": me_f, "head": 1 - me_s},
            device_id_type=MESH,
        )

    def space_mix(p, g, c):
        def store(m, j, part):
            qv[j, pl.ds(pl.multiple_of(m * step, step), step), :] = part

        project_pair(0, p, (g, first_slot(g)), (g, second_slot(g)), store)

        @pl.when(me_f > 0)
        def _():
            near_copy(0, g).wait_recv()

        @pl.when(me_f < frames - 1)
        def _():
            near_copy(1, g).wait_recv()

        def one(j, c):
            h = 2 * g + j
            for n, ref in ((0, ka), (1, va)):
                ref[:rows, :HD] = kv[n, h].reshape(rows, HD)
                ref[rows : rows + near, :HD] = nrecv[0, g, n, j].reshape(near, HD)
                ref[rows + near :, :HD] = nrecv[1, g, n, j].reshape(near, HD)
            for b in range(total // BLOCK):
                ka[b * BLOCK : (b + 1) * BLOCK, HD:] = jnp.broadcast_to(
                    bias_ref[h, b : b + 1, :], (BLOCK, HD)
                ).astype(jnp.bfloat16)
            part = rows // sides
            size = chunk_rows(part, 256)
            for m in range(rows // size):
                span = slice(m * size, (m + 1) * size)
                queries = jnp.concatenate([qv[j, span, :], marks[span, :]], axis=1)
                result = attend_rows(queries, ka[...], va[...], factor)
                which = lax.rem(m * size // part - me_s + sides, sides)
                first = m * size % part
                sout[which, h, first : first + size, :] = result
            return c

        lax.fori_loop(0, 2, one, 0)
        own_copy(g).start()
        other_copy(g).start()
        return c

    def time_mix(p):
        for kind in range(3):
            pltpu.make_async_copy(trecv.at[p, kind], trecv.at[p, kind], t_recv.at[p, kind]).wait()
        span = pos * (BLOCK // STRIP)

        def one(j, c):
            head = 2 * p + j
            ka[:rows, :HD] = trecv[p, 1, :, j].reshape(rows, HD)
            va[:rows, :HD] = trecv[p, 2, :, j].reshape(rows, HD)
            strip = lax.rem(row, pos) // STRIP
            block = row // span
            lane_strip, lane_block = lane // blocks, lax.rem(lane, blocks)
            live = jnp.zeros((rows, HD), jnp.float32)
            for a in range(blocks):
                for b in range(blocks):
                    m = table[mask_at + (head * blocks + a) * blocks + b].astype(jnp.float32)
                    live = jnp.where((lane_block == a) & (block == b), m, live)
            live = jnp.where(strip == lane_strip, live, 0.0)
            ka[:rows, HD:] = ((live - 1.0) * BIG).astype(jnp.bfloat16)
            tags = jnp.where(strip * blocks + block == lane, 1.0, 0.0).astype(jnp.bfloat16)
            queries = jnp.concatenate([trecv[p, 0, :, j].reshape(rows, HD), tags], axis=1)
            size = chunk_rows(rows, 256)
            per = size // pos
            for m in range(rows // size):
                result = attend_rows(queries[m * size : (m + 1) * size], ka[:rows], va[:rows], factor)
                tout[p, m * per * sides : (m + 1) * per * sides, j] = result.reshape(per * sides, q, HD)
            return c

        lax.fori_loop(0, 2, one, 0)
        heads = pl.ds(2 * p, 2)
        pltpu.make_async_copy(tout.at[p, me], back_hbm.at[me_f, me_s, heads], r_recv.at[p]).start()

        def send(i, c):
            to = lax.rem(me + spread(i, devices), devices)
            pltpu.make_async_remote_copy(
                src_ref=tout.at[p, to],
                dst_ref=back_hbm.at[me_f, me_s, heads],
                send_sem=r_send.at[p],
                recv_sem=r_recv.at[p],
                device_id={"frame": to // sides, "head": lax.rem(to, sides)},
                device_id_type=MESH,
            ).start()
            return c

        lax.fori_loop(0, devices - 1, send, 0)

    time_project(0, True)
    for p in range(1, pairs):
        time_project(p, False)
    for p in range(pairs):
        lax.fori_loop(2 * p, 2 * p + 2, functools.partial(space_project, p), 0)
    for p in range(pairs):
        lax.fori_loop(2 * p, 2 * p + 2, functools.partial(space_mix, p), 0)
        time_mix(p)

    def drain(g, c):
        own_copy(g).wait()
        other_copy(g).wait()

        @pl.when(me_f < frames - 1)
        def _():
            near_copy(0, g).wait_send()

        @pl.when(me_f > 0)
        def _():
            near_copy(1, g).wait_send()

        return c

    lax.fori_loop(0, groups, drain, 0)
    for p in range(pairs):
        for kind in range(3):
            sent = tsend.at[p, kind, pl.ds(0, frames - 1)]
            pltpu.make_async_copy(sent, sent, t_send.at[p, kind]).wait()
        sent = tout.at[p, pl.ds(0, devices - 1)]
        pltpu.make_async_copy(sent, sent, r_send.at[p]).wait()
        pltpu.make_async_copy(tout.at[p], tout.at[p], r_recv.at[p]).wait()
    labels_copy.wait()


def fused(tokens, weight, gq, gk, table, slots_row, picks, bias, blocks):
    rows, d = tokens.shape
    frames = lax.axis_size("frame")
    sides = lax.axis_size("head")
    heads = bias.shape[0]
    groups = heads // 2
    pairs = groups // 2
    near = NEAR_MAX * BLOCK
    total = rows + 2 * near
    pos = rows // frames
    q = pos // sides
    part = rows // sides
    bf = jnp.bfloat16
    any_spec = pl.BlockSpec(memory_space=pl.ANY)
    vmem_spec = pl.BlockSpec(memory_space=pltpu.VMEM)
    smem_spec = pl.BlockSpec(memory_space=pltpu.SMEM)
    dma = pltpu.SemaphoreType.DMA
    return pl.pallas_call(
        functools.partial(fused_kernel, math.log2(math.e) / math.sqrt(HD), blocks),
        out_shape=(
            jax.ShapeDtypeStruct((heads, part, HD), bf),
            jax.ShapeDtypeStruct((heads, part, HD), bf),
            jax.ShapeDtypeStruct((frames, sides, groups, q, HD), bf),
            jax.ShapeDtypeStruct((1, HD), jnp.int32),
        ),
        in_specs=[smem_spec, smem_spec, vmem_spec, vmem_spec, vmem_spec, any_spec, any_spec, any_spec],
        out_specs=(any_spec,) * 4,
        scratch_shapes=[
            pltpu.VMEM((rows, d), bf),
        ]
        + [pltpu.VMEM((groups // 2, 3, d, HD), bf)] * 6
        + [
            pltpu.VMEM((pairs, 3, frames, 2, pos, HD), bf),
            pltpu.VMEM((pairs, 3, frames, 2, pos, HD), bf),
            pltpu.VMEM((2, heads, rows // BLOCK, BLOCK, HD), bf),
            pltpu.VMEM((2, groups, 2, 2, NEAR_MAX, BLOCK, HD), bf),
            pltpu.VMEM((2, groups, 2, 2, NEAR_MAX, BLOCK, HD), bf),
            pltpu.VMEM((2, rows, HD), bf),
            pltpu.VMEM((total, 2 * HD), bf),
            pltpu.VMEM((total, 2 * HD), bf),
            pltpu.VMEM((rows, HD), bf),
            pltpu.VMEM((sides, heads, part, HD), bf),
            pltpu.VMEM((pairs, frames * sides, 2, q, HD), bf),
            dma((sides,)),
            dma((3, groups, 3)),
            dma((pairs, 3)),
            dma((pairs, 3)),
            dma((2, groups)),
            dma((2, groups)),
            dma((groups,)),
            dma((groups,)),
            dma((groups,)),
            dma((pairs,)),
            dma((pairs,)),
            dma,
            dma,
        ],
        compiler_params=pltpu.CompilerParams(
            vmem_limit_bytes=FUSED_VMEM, collective_id=0, has_side_effects=True
        ),
        name="fused",
    )(table, picks, bias, gq, gk, tokens, weight, slots_row)


def tables_kernel(tblocks, labels_ref, time_ref, mask_ref, scalars_ref, slots_ref, picks_ref, bias_ref):
    frames = lax.axis_size("frame")
    me_f = lax.axis_index("frame")
    count, blocks, wide = mask_ref.shape
    groups = count // 3
    near = NEAR_MAX
    keys = blocks + 2 * near
    low_ok = (me_f > 0).astype(jnp.float32)
    high_ok = (me_f < frames - 1).astype(jnp.float32)
    row = lax.broadcasted_iota(jnp.int32, (keys, wide), 0)
    lane = lax.broadcasted_iota(jnp.int32, (keys, wide), 1)
    side = jnp.where(row < blocks + near, 0, 1)
    want = jnp.where(row < blocks, -1, row - blocks - side * near).astype(jnp.float32)
    own = jnp.where(lane - blocks == row, 1.0, 0.0) * jnp.where(row < blocks, 1.0, 0.0)
    ok = jnp.where(row < blocks, 1.0, jnp.where(side == 0, low_ok, high_ok))[:, :1]
    inside = jnp.where(lane // blocks == side * 2, 1.0, 0.0)
    before = lax.broadcasted_iota(jnp.int32, (wide, wide), 0)
    after = lax.broadcasted_iota(jnp.int32, (wide, wide), 1)
    earlier = jnp.where((before < after) & (before // blocks == after // blocks), 1.0, 0.0).astype(jnp.bfloat16)
    name = lax.rem(lane, blocks).astype(jnp.float32)
    bias_ref[...] = jnp.zeros(bias_ref.shape, bias_ref.dtype)
    picks_ref[...] = jnp.zeros(picks_ref.shape, picks_ref.dtype)
    for g in range(groups):
        slot = labels_ref[3 * g + 1] + 2 * labels_ref[3 * g + 2]
        first = jnp.where(slot == 0, 1, 0)
        second = jnp.where(slot == 2, 1, 2)
        scalars_ref[g] = slot
        scalars_ref[groups + g] = first
        scalars_ref[2 * groups + g] = second
        slots_ref[0, g] = slot
        for a in range(tblocks):
            for b in range(tblocks):
                at = 3 * groups + (g * tblocks + a) * tblocks + b
                scalars_ref[at] = time_ref[((3 * g + slot) * tblocks + a) * tblocks + b]
        for j, which in ((0, first), (1, second)):
            live = mask_ref[3 * g + which].astype(jnp.float32)
            used = jnp.max(live, axis=0, keepdims=True)
            used = jnp.broadcast_to(used, (8, wide))
            rank = jnp.dot(used.astype(jnp.bfloat16), earlier, preferred_element_type=jnp.float32)
            chosen = jnp.where(rank[:1] == want, 1.0, 0.0) * used[:1] * inside
            select = own + chosen
            allowed = lax.dot_general(
                select.astype(jnp.bfloat16),
                live.astype(jnp.bfloat16),
                (((1,), (1,)), ((), ())),
                preferred_element_type=jnp.float32,
            )
            h = 2 * g + j
            bias_ref[h, :, :blocks] = (allowed * ok - 1.0) * BIG
            number = lax.dot_general(
                name[:8].astype(jnp.bfloat16),
                chosen.astype(jnp.bfloat16),
                (((1,), (1,)), ((), ())),
                preferred_element_type=jnp.float32,
            )
            picks_ref[h : h + 1, :keys] = number[:1].astype(jnp.int32)


def tables(labels, time_mask, space_mask):
    groups = labels.shape[0] // 3
    blocks = space_mask.shape[1]
    tblocks = time_mask.shape[1]
    keys = blocks + 2 * NEAR_MAX
    smem = pl.BlockSpec(memory_space=pltpu.SMEM)
    vmem = pl.BlockSpec(memory_space=pltpu.VMEM)
    return pl.pallas_call(
        functools.partial(tables_kernel, tblocks),
        out_shape=(
            jax.ShapeDtypeStruct((groups * (3 + tblocks * tblocks),), jnp.int32),
            jax.ShapeDtypeStruct((1, HD), jnp.int32),
            jax.ShapeDtypeStruct((2 * groups, HD), jnp.int32),
            jax.ShapeDtypeStruct((2 * groups, keys, HD), jnp.float32),
        ),
        in_specs=[smem, smem, vmem],
        out_specs=(smem, smem, vmem, vmem),
        name="tables",
    )(labels, time_mask.reshape(-1), space_mask)


def place_kernel(mine_ref, theirs_ref, own_ref, other_ref, back_ref, out_ref):
    side = lax.axis_index("head")
    groups = back_ref.shape[2]
    rows = out_ref.shape[0]

    def put(head, value):
        out_ref[:, pl.ds(pl.multiple_of(head * HD, HD), HD)] = value

    for g in range(groups):
        for whose, slots, ref in ((side, mine_ref, own_ref), (1 - side, theirs_ref, other_ref)):
            slot = slots[0, g]
            base = 3 * (whose * groups + g)
            put(base + jnp.where(slot == 0, 1, 0), ref[2 * g])
            put(base + jnp.where(slot == 2, 1, 2), ref[2 * g + 1])
            put(base + slot, back_ref[:, whose, g].reshape(rows, HD))


def place(mine, theirs, own, other, back):
    heads, rows, _ = own.shape
    _, sides, groups, q, _ = back.shape
    size = chunk_rows(rows, 128)
    scalar = pl.BlockSpec(memory_space=pltpu.SMEM)
    space = pl.BlockSpec((heads, size, HD), lambda i: (0, i, 0))
    return pl.pallas_call(
        place_kernel,
        out_shape=jax.ShapeDtypeStruct((rows, sides * groups * 3 * HD), jnp.bfloat16),
        grid=(rows // size,),
        in_specs=[
            scalar,
            scalar,
            space,
            space,
            pl.BlockSpec((size // q, sides, groups, q, HD), lambda i: (i, 0, 0, 0, 0)),
        ],
        out_specs=pl.BlockSpec((size, sides * groups * 3 * HD), lambda i: (i, 0)),
        name="place",
    )(mine, theirs, own, other, back)


def block_picks(live):
    used = jnp.max(live, axis=1)
    width = used.shape[1]
    before = (jnp.arange(width)[:, None] < jnp.arange(width)[None, :]).astype(jnp.int32)
    rank = jnp.sum(used[:, :, None] * before[None], axis=1)
    return used[:, None, :] * (rank[:, None, :] == jnp.arange(NEAR_MAX)[None, :, None]).astype(jnp.int32)


def on_device(tokens, qkv_weight, query_gain, key_gain, labels, space_mask, time_mask):
    frame_count = lax.axis_size("frame")
    sides = lax.axis_size("head")
    own_frame = lax.axis_index("frame")
    own_side = lax.axis_index("head")
    row_count = tokens.shape[0]
    groups = labels.shape[0] // 3
    blocks = row_count // BLOCK
    space_count = 2 * groups
    gq, gk = query_gain.reshape(1, HD), key_gain.reshape(1, HD)

    pos_count = row_count // frame_count
    deal = sides if pos_count % (sides * STRIP) == 0 else 1
    if sides == 2 and deal == 2 and groups == 4:
        table, mine, picks, bias = tables(labels, time_mask, space_mask)
        own_out, other_out, back, theirs = fused(
            tokens, qkv_weight, gq, gk, table, mine, picks, bias, time_mask.shape[1]
        )
        return place(mine, theirs, own_out, other_out, back)

    picked = labels.reshape(groups, 3)
    time_slot = jnp.sum(picked * jnp.arange(3, dtype=jnp.int32)[None, :], axis=1)
    group_base = 3 * jnp.arange(groups, dtype=jnp.int32)
    time_heads = group_base + time_slot
    first_space = group_base + jnp.where(time_slot == 0, 1, 0)
    second_space = group_base + jnp.where(time_slot == 2, 1, 2)
    space_heads = jnp.stack([first_space, second_space], axis=1).reshape(space_count)

    live = jnp.take(space_mask, space_heads, axis=0)
    low, own, high = live[:, :, :blocks], live[:, :, blocks : 2 * blocks], live[:, :, 2 * blocks :]
    low_pick, high_pick = block_picks(low), block_picks(high)
    ids = jnp.arange(blocks, dtype=jnp.int32)
    picks = jnp.stack([jnp.sum(low_pick * ids, axis=-1), jnp.sum(high_pick * ids, axis=-1)], axis=1)
    low_ok = (own_frame > 0).astype(jnp.int32)
    high_ok = (own_frame < frame_count - 1).astype(jnp.int32)

    def near_live(pick, side, ok):
        return ok * jnp.sum(pick[:, :, None, :] * side[:, None, :, :], axis=-1)

    allowed = jnp.concatenate(
        [jnp.swapaxes(own, 1, 2), near_live(low_pick, low, low_ok), near_live(high_pick, high, high_ok)],
        axis=1,
    )
    bias = jnp.pad((allowed.astype(jnp.float32) - 1.0) * BIG, ((0, 0), (0, 0), (0, HD - blocks)))

    up = [(i, i + 1) for i in range(frame_count - 1)]
    down = [(i + 1, i) for i in range(frame_count - 1)]
    swap = [(0, 1), (1, 0)]
    kv, to_next, to_prev = project(tokens, qkv_weight, gq, gk, space_heads, (1, 2), gq, picks=picks)
    prev_kv = lax.ppermute(to_next, "frame", up)
    next_kv = lax.ppermute(to_prev, "frame", down)
    packed = project(
        tokens, qkv_weight, gq, gk, time_heads, (0, 1, 2), kv, strips=frame_count, deal=deal
    )
    received = lax.all_to_all(packed, "frame", split_axis=0, concat_axis=0, tiled=True)
    query_heads = space_heads
    if sides == 2:
        their_slot = lax.ppermute(time_slot, "head", swap)
        query_heads, their_slot = lax.optimization_barrier((space_heads, their_slot))
        slots = jnp.where(
            own_side == 0,
            jnp.concatenate([time_slot, their_slot]),
            jnp.concatenate([their_slot, time_slot]),
        )
    else:
        slots = lax.all_to_all(
            jnp.broadcast_to(time_slot[None], (sides, groups)), "head", 0, 0, tiled=True
        ).reshape(-1)
    space_q = project(tokens, qkv_weight, gq, gk, query_heads, (0,), packed)

    side = jnp.reshape(own_side if sides == 2 else jnp.int32(0), (1,)).astype(jnp.int32)
    space_out = space_attend(space_q, kv, prev_kv, next_kv, bias, sides, side, space_q)
    mask = jnp.take(time_mask, time_heads, axis=0)
    time_out = time_attend(received, mask, space_out, deal)

    part_rows = row_count // sides
    total_heads = sides * space_count
    head_ids = jnp.arange(total_heads, dtype=jnp.int32)
    if sides == 2:
        space_recv = lax.ppermute(space_out[1], "head", swap)

        def clamped(whose):
            return jnp.clip(head_ids - whose * space_count, 0, space_count - 1)

        sources = [(space_out[0], clamped(own_side)), (space_recv, clamped(1 - own_side))]
        chosen = (head_ids // space_count != own_side).astype(jnp.int32)
    else:
        space_all = lax.all_to_all(space_out, "head", 0, 0, tiled=True)
        sources = [(space_all.reshape(total_heads, part_rows, HD), head_ids)]
        chosen = jnp.zeros_like(head_ids)
    all_groups = jnp.arange(sides * groups, dtype=jnp.int32)
    firsts = 3 * all_groups + jnp.where(slots == 0, 1, 0)
    seconds = 3 * all_groups + jnp.where(slots == 2, 1, 2)
    space_columns = jnp.stack([firsts, seconds], axis=1).reshape(total_heads)
    placed = place_space(space_columns, chosen, sources, sides * groups * 3 * HD)

    if deal == sides:
        q = pos_count // sides
        timed = lax.all_to_all(
            time_out.reshape(frame_count * sides, groups, q, HD), ("frame", "head"), 0, 0, tiled=True
        )
        timed = timed.reshape(frame_count, sides, groups, q, HD)

        def pick(ref, g):
            return ref[:, g // groups, g % groups]

    else:
        timed = time_out.reshape(frame_count, groups, pos_count, HD)
        timed = lax.all_to_all(timed, "frame", 0, 0, tiled=True)
        timed = lax.all_to_all(timed, "head", 0, 0, tiled=True)
        timed = timed.reshape(sides, frame_count // sides, groups, pos_count, HD)

        def pick(ref, g):
            return ref[g // groups, :, g % groups]

    return place_time(3 * all_groups + slots, timed, pick, placed)


def solution(mesh):
    placed = (
        P("frame", None),
        P(None, None, "head"),
        P(),
        P(),
        P("head"),
        P("head", None, None),
        P("head", None, None),
    )

    return jax.shard_map(
        on_device, mesh=mesh, in_specs=placed, out_specs=P(("frame", "head"), None), check_vma=False
    )
```
